32 devices in a mesh: sub: 8 (over y, x, core), row: 4 (over z).
Axes of the slice: x: 2, y: 2, z: 4, core: 2. Of those that a mesh axis runs over, the one named last changes fastest.
Arguments:
- basis: bfloat16 [8, 49152, 128], P('sub', 'row'), may hold values from -0.40234375 to 0.40234375
- local_operator: bfloat16 [8, 49152, 384], P('sub', 'row'), may hold values from -0.3125 to 0.3125
- coupling: bfloat16 [3, 8, 4, 2, 128, 128], P(None, 'sub', 'row'), may hold values from -0.5 to 0.5
- partners: int32 [3, 8], replicated, may hold values from 0 to 7, as said below
- margin_blocks: int32 [3, 8, 4, 2], P(None, 'sub', 'row'), may hold values from 0 to 95, as said below
Outputs:
- coarse_tiles: float32 [8, 4, 128, 128], P('sub', None, 'row')
The draws below stay inside these ranges and needn't reach their ends.
Inputs may be any that keep to these rules, and one draw needn't show every extreme that they name: In every round the partners form a perfect matching: partners[r, partners[r, s]] = s and partners[r, s] != s. `margin_blocks`: for each round, subdomain and device row the 2 entries are different row blocks of that device.
All inputs are finite; a program needn't handle non-finite values.
Results may differ from the reference program's by a relative error of at most 0.0003.
Values may be sent and summed in bfloat16 or wider, within the bound.
A program may use at most 128 MiB of HBM per device.

```python
import jax
import jax.numpy as jnp
from jax import lax

K = 128
BLK = 128
OVL = 2
ROUNDS = 3
ROWS_DEV = 12288
SUBS = 8
ROWS = 49152
NBLK = 96
N_ROW = 4


def draw_partners(key, part):
    rows = []
    for turn in range(ROUNDS):
        order = jax.random.permutation(jax.random.fold_in(key, turn), SUBS).astype(jnp.int32)
        first = order[0::2]
        second = order[1::2]
        mate = jnp.zeros((SUBS,), jnp.int32).at[first].set(second).at[second].set(first)
        rows.append(mate)
    return jnp.stack(rows, axis=0)


def draw_margin_blocks(key, part):
    nrow = ROWS // ROWS_DEV
    total = ROUNDS * SUBS * nrow
    keys = jax.random.split(jax.random.fold_in(key, 11), total)
    picks = jax.vmap(lambda k: jax.random.permutation(k, NBLK)[:OVL])(keys).astype(jnp.int32)
    picks = picks.at[0].set(jnp.arange(NBLK - OVL, NBLK, dtype=jnp.int32))
    return picks.reshape(ROUNDS, SUBS, nrow, OVL)


def block_levels(own_key, shape, pieces, smallest, high):
    def one(position, shards_of):
        steps = jax.random.uniform(jax.random.fold_in(jax.random.fold_in(own_key, 6), position), (shards_of,), jnp.float32, smallest / len(pieces), high / len(pieces))
        return jnp.repeat(jnp.exp(steps), shape[position] // shards_of).reshape((-1,) + (1,) * (len(shape) - position - 1))

    gain = one(*pieces[0])
    for cut in pieces[1:]:
        gain = gain * one(*cut)
    return gain


def gaussian(key, extent, width, reach, cuts=(), kind=jnp.bfloat16):
    entries = width * jax.random.normal(key, extent, jnp.float32)
    if cuts:
        entries = entries * block_levels(key, extent, cuts, -0.22, 0.18)
    return jnp.clip(entries, -reach, reach).astype(kind)


def setup_inputs(seed: int = 0) -> dict:
    key_list = jax.random.split(jax.random.key(seed), 6)
    return {
        "basis": gaussian(key_list[0], (SUBS, ROWS, K), (ROWS ** -0.25), 0.40234375, ((0, 8), (1, 4))),
        "local_operator": gaussian(key_list[1], (SUBS, ROWS, 3 * BLK), (3 * BLK) ** -0.5, 0.3125, ((0, 8), (1, 4))),
        "coupling": gaussian(key_list[2], (ROUNDS, SUBS, N_ROW, OVL, BLK, BLK), BLK ** -0.5, 0.5, ((1, 8), (2, 4))),
        "partners": draw_partners(jax.random.fold_in(key_list[5], 71), 0),
        "margin_blocks": draw_margin_blocks(jax.random.fold_in(key_list[5], 71), 0),
    }


def diagonal_tile(zsub, gsub):
    count = zsub.shape[0] // BLK
    zf = zsub.astype(jnp.float32)
    blocks = zf.reshape(count, BLK, K)
    padded = jnp.pad(blocks, ((1, 1), (0, 0), (0, 0)))
    stacked = jnp.stack([padded[:-2], padded[1:-1], padded[2:]], axis=1)
    gmat = gsub.astype(jnp.float32).reshape(count, BLK, 3, BLK)
    image = jnp.einsum("mioj,mojk->mik", gmat, stacked, precision=lax.Precision.HIGHEST)
    return jnp.dot(zf.T, image.reshape(zsub.shape[0], K), precision=lax.Precision.HIGHEST)


def reference(basis, local_operator, coupling, partners, margin_blocks):
    diag = lax.map(lambda pair: diagonal_tile(pair[0], pair[1]), (basis, local_operator))
    nrow = ROWS // ROWS_DEV
    zr = basis.reshape(SUBS, nrow, ROWS_DEV // BLK, BLK, K)
    sidx = jnp.arange(SUBS, dtype=jnp.int32)[None, :, None, None]
    qidx = jnp.arange(nrow, dtype=jnp.int32)[None, None, :, None]
    own = zr[sidx, qidx, margin_blocks.astype(jnp.int32)].astype(jnp.float32)
    ridx = jnp.arange(ROUNDS, dtype=jnp.int32)[:, None]
    other = own[ridx, partners.astype(jnp.int32)]
    moved = jnp.einsum("rsqbij,rsqbjl->rsqbil", coupling.astype(jnp.float32), other, precision=lax.Precision.HIGHEST)
    offdiag = jnp.einsum("rsqbik,rsqbil->rskl", own, moved, precision=lax.Precision.HIGHEST)
    return jnp.concatenate([diag[:, None], jnp.transpose(offdiag, (1, 0, 2, 3))], axis=1)
```

```python
import functools

import jax
import jax.numpy as jnp
from jax import lax
from jax.experimental import pallas as pl
from jax.experimental.pallas import tpu as pltpu
from jax.sharding import PartitionSpec as P

MESH = pl.DeviceIdType.MESH
GROUP = 4
TN = (((0,), (0,)), ((), ()))


def split(value):
    high = value.astype(jnp.bfloat16)
    low = (value - high.astype(jnp.float32)).astype(jnp.bfloat16)
    return jnp.concatenate([high, low], axis=1)


def kernel(
    nsub, nrow, partners, margins, basis, operator, coupling, out,
    zpad, gbuf, cbuf, halo, gath, outbox, inbox, acc,
    dsend, osend, drecv, orecv,
    zsem, gsem, csem, hsend, hrecv, psend, precv, bsend, brecv,
    dss, dsr, oss, osr,
):
    sub = lax.axis_index("sub")
    row = lax.axis_index("row")
    chips = nsub // 2
    chip = sub // 2
    core = sub % 2
    mate = chip * 2 + (1 - core)
    count = basis.shape[0]
    groups = count // GROUP
    rounds = margins.shape[0]
    ovl = margins.shape[1]
    share = out.shape[1]
    blk = basis.shape[1]
    width = basis.shape[2]

    def zcopy(g):
        return pltpu.make_async_copy(
            basis.at[pl.ds(g * GROUP, GROUP)], zpad.at[pl.ds(g * GROUP + 1, GROUP)], zsem.at[g]
        )

    def gcopy(g):
        return pltpu.make_async_copy(
            operator.at[pl.ds(g * GROUP, GROUP)], gbuf.at[pl.ds(g * GROUP, GROUP)], gsem.at[g]
        )

    ccopy = pltpu.make_async_copy(coupling, cbuf, csem)

    def each(lower, upper, body):
        lax.fori_loop(lower, upper, lambda i, _: (body(i), 0)[1], 0)

    each(0, groups, lambda g: zcopy(g).start())
    each(0, groups, lambda g: gcopy((g + 1) % groups).start())
    ccopy.start()

    barrier = pltpu.get_barrier_semaphore()
    for step in range(1, chips):
        peer = ((chip + step) % chips) * 2 + core
        pl.semaphore_signal(barrier, inc=1, device_id=(peer, row), device_id_type=MESH)
    pl.semaphore_signal(barrier, inc=1, device_id=(mate, row), device_id_type=MESH)
    for step in range(1, nrow):
        pl.semaphore_signal(
            barrier, inc=1, device_id=(sub, (row + step) % nrow), device_id_type=MESH
        )
    pl.semaphore_wait(barrier, chips + nrow - 1)

    up = pltpu.make_async_remote_copy(
        basis.at[count - 1], halo.at[0], hsend.at[0], hrecv.at[0],
        device_id=(sub, (row + 1) % nrow), device_id_type=MESH,
    )
    down = pltpu.make_async_remote_copy(
        basis.at[0], halo.at[1], hsend.at[1], hrecv.at[1],
        device_id=(sub, (row + nrow - 1) % nrow), device_id_type=MESH,
    )

    @pl.when(row < nrow - 1)
    def _():
        up.start()

    @pl.when(row > 0)
    def _():
        down.start()

    each(0, groups, lambda g: zcopy(g).wait())
    for turn in range(rounds):
        for b in range(ovl):
            gath[chip, turn * ovl + b] = zpad[margins[turn, b] + 1]

    def packet(step):
        return pltpu.make_async_remote_copy(
            gath.at[chip], gath.at[chip], psend.at[step], precv.at[step],
            device_id=(((chip + step) % chips) * 2 + core, row), device_id_type=MESH,
        )

    def arrival(step):
        source = (chip + chips - step) % chips
        return pltpu.make_async_remote_copy(
            gath.at[source], gath.at[source], psend.at[step], precv.at[step],
            device_id=(source * 2 + core, row), device_id_type=MESH,
        )

    for step in range(1, chips):
        packet(step).start()

    acc[...] = jnp.zeros_like(acc)

    def work(g):
        first = g * GROUP
        parts = []
        for j in range(GROUP):
            near = zpad[pl.ds(first + j, 3)].reshape(3 * blk, width)
            image = jnp.dot(gbuf[first + j], near, preferred_element_type=jnp.float32)
            parts.append(split(image))
        own = zpad[pl.ds(first + 1, GROUP)].reshape(GROUP * blk, width)
        acc[...] += lax.dot_general(
            own, jnp.concatenate(parts, axis=0), TN, preferred_element_type=jnp.float32
        )

    def middle(g):
        gcopy(g).wait()
        work(g)

    each(1, groups - 1, middle)

    @pl.when(row > 0)
    def _():
        up.wait_recv()
        zpad[0] = halo[0]

    @pl.when(row == 0)
    def _():
        zpad[0] = jnp.zeros((blk, width), jnp.bfloat16)

    @pl.when(row < nrow - 1)
    def _():
        down.wait_recv()
        zpad[count + 1] = halo[1]

    @pl.when(row == nrow - 1)
    def _():
        zpad[count + 1] = jnp.zeros((blk, width), jnp.bfloat16)

    each(0, 2, lambda i: middle(i * (groups - 1)))

    tile = acc[:, :width] + acc[:, width:]
    dsend[...] = tile.reshape(nrow, share, width)

    def share_out(step, source, target, ss, sr):
        there = (row + step) % nrow
        return pltpu.make_async_remote_copy(
            source.at[there], target.at[step - 1], ss.at[step - 1], sr.at[step - 1],
            device_id=(sub, there), device_id_type=MESH,
        )

    for step in range(1, nrow):
        share_out(step, dsend, drecv, dss, dsr).start()

    for step in range(1, chips):
        arrival(step).wait_recv()
    for turn in range(rounds):
        wanted = partners[turn, mate] // 2
        for b in range(ovl):
            outbox[turn * ovl + b] = gath[wanted, turn * ovl + b]
    cross = pltpu.make_async_remote_copy(
        outbox, inbox, bsend, brecv, device_id=(mate, row), device_id_type=MESH
    )
    cross.start()
    ccopy.wait()
    cross.wait_recv()
    for turn in range(rounds):
        wanted = partners[turn, sub]
        here = jnp.full((blk, width), wanted % 2, jnp.int32) == core
        parts = []
        for b in range(ovl):
            k = turn * ovl + b
            near = gath[wanted // 2, k].astype(jnp.float32)
            far = inbox[k].astype(jnp.float32)
            other = jnp.where(here, near, far).astype(jnp.bfloat16)
            parts.append(split(jnp.dot(cbuf[k], other, preferred_element_type=jnp.float32)))
        own = gath[chip, pl.ds(turn * ovl, ovl)].reshape(ovl * blk, width)
        both = lax.dot_general(
            own, jnp.concatenate(parts, axis=0), TN, preferred_element_type=jnp.float32
        )
        osend[:, turn] = (both[:, :width] + both[:, width:]).reshape(nrow, share, width)
    for step in range(1, nrow):
        share_out(step, osend, orecv, oss, osr).start()

    total = dsend[row]
    for step in range(1, nrow):
        share_out(step, dsend, drecv, dss, dsr).wait_recv()
        total += drecv[step - 1]
    out[0] = total
    total = osend[row]
    for step in range(1, nrow):
        share_out(step, osend, orecv, oss, osr).wait_recv()
        total += orecv[step - 1]
    out[1:] = total

    @pl.when(row < nrow - 1)
    def _():
        up.wait_send()

    @pl.when(row > 0)
    def _():
        down.wait_send()

    for step in range(1, chips):
        packet(step).wait_send()
    cross.wait_send()
    for step in range(1, nrow):
        share_out(step, dsend, drecv, dss, dsr).wait_send()
        share_out(step, osend, orecv, oss, osr).wait_send()


def local(nsub, nrow, basis, local_operator, coupling, partners, margin_blocks):
    rounds, _, _, ovl, blk, _ = coupling.shape
    rows, width = basis.shape[1:]
    count = rows // blk
    groups = count // GROUP
    share = width // nrow
    chips = nsub // 2
    bf16, f32 = jnp.bfloat16, jnp.float32
    dma = pltpu.SemaphoreType.DMA
    any_space = pl.BlockSpec(memory_space=pl.ANY)
    smem = pl.BlockSpec(memory_space=pltpu.SMEM)
    out = pl.pallas_call(
        functools.partial(kernel, nsub, nrow),
        out_shape=jax.ShapeDtypeStruct((1 + rounds, share, width), f32),
        in_specs=[smem, smem, any_space, any_space, any_space],
        out_specs=pl.BlockSpec(memory_space=pltpu.VMEM),
        scratch_shapes=[
            pltpu.VMEM((count + 2, blk, width), bf16),
            pltpu.VMEM((count, blk, 3 * blk), bf16),
            pltpu.VMEM((rounds * ovl, blk, blk), bf16),
            pltpu.VMEM((2, blk, width), bf16),
            pltpu.VMEM((chips, rounds * ovl, blk, width), bf16),
            pltpu.VMEM((rounds * ovl, blk, width), bf16),
            pltpu.VMEM((rounds * ovl, blk, width), bf16),
            pltpu.VMEM((width, 2 * width), f32),
            pltpu.VMEM((nrow, share, width), f32),
            pltpu.VMEM((nrow, rounds, share, width), f32),
            pltpu.VMEM((nrow - 1, share, width), f32),
            pltpu.VMEM((nrow - 1, rounds, share, width), f32),
            dma((groups,)), dma((groups,)), dma(()), dma((2,)), dma((2,)),
            dma((chips,)), dma((chips,)), dma(()), dma(()),
            dma((nrow - 1,)), dma((nrow - 1,)), dma((nrow - 1,)), dma((nrow - 1,)),
        ],
        compiler_params=pltpu.CompilerParams(
            collective_id=0, has_side_effects=True, vmem_limit_bytes=56 << 20
        ),
        name="coarse",
    )(
        partners,
        margin_blocks.reshape(rounds, ovl),
        basis.reshape(count, blk, width),
        local_operator.reshape(count, blk, 3 * blk),
        coupling.reshape(rounds * ovl, blk, blk),
    )
    return out[None]


def solution(mesh):
    placed = (
        P("sub", "row", None),
        P("sub", "row", None),
        P(None, "sub", "row", None, None, None),
        P(),
        P(None, "sub", "row", None),
    )
    body = functools.partial(local, mesh.shape["sub"], mesh.shape["row"])
    return jax.shard_map(
        body, mesh=mesh, in_specs=placed, out_specs=P("sub", None, "row", None), check_vma=False
    )
```

```python
import functools

import jax
import jax.numpy as jnp
from jax import lax
from jax.experimental import pallas as pl
from jax.experimental.pallas import tpu as pltpu
from jax.sharding import PartitionSpec as P

MESH = pl.DeviceIdType.MESH
GROUP = 8
MARKS = (7, 8, 9, 10, 10)
TN = (((0,), (0,)), ((), ()))


def split(value):
    high = value.astype(jnp.bfloat16)
    low = (value - high.astype(jnp.float32)).astype(jnp.bfloat16)
    return jnp.concatenate([high, low], axis=1)


def kernel(
    nsub, nrow, partners, margins, basis, operator, coupling, out,
    zpad, gbuf, cbuf, halo, gath, outbox, inbox, acc,
    tsend, trecv,
    zsem, gsem, csem, hsend, hrecv, psend, precv, bsend, brecv,
    tss, tsr,
):
    sub = lax.axis_index("sub")
    row = lax.axis_index("row")
    chips = nsub // 2
    chip = sub // 2
    core = sub % 2
    mate = chip * 2 + (1 - core)
    count = basis.shape[0]
    groups = count // GROUP
    rounds = margins.shape[1]
    ovl = margins.shape[0]
    share = out.shape[1]
    blk = basis.shape[1]
    width = basis.shape[2]

    def zcopy(g):
        return pltpu.make_async_copy(
            basis.at[pl.ds(g * GROUP, GROUP)], zpad.at[pl.ds(g * GROUP + 1, GROUP)], zsem.at[g]
        )

    def gcopy(g):
        return pltpu.make_async_copy(
            operator.at[pl.ds(g * GROUP, GROUP)], gbuf.at[pl.ds(g * GROUP, GROUP)], gsem.at[g]
        )

    ccopy = pltpu.make_async_copy(coupling, cbuf, csem)

    def each(lower, upper, body):
        lax.fori_loop(lower, upper, lambda i, _: (body(i), 0)[1], 0)

    barrier = pltpu.get_barrier_semaphore()
    for step in range(1, chips):
        peer = ((chip + step) % chips) * 2 + core
        pl.semaphore_signal(barrier, inc=1, device_id=(peer, row), device_id_type=MESH)
    pl.semaphore_signal(barrier, inc=1, device_id=(mate, row), device_id_type=MESH)
    for step in range(1, nrow):
        pl.semaphore_signal(
            barrier, inc=1, device_id=(sub, (row + step) % nrow), device_id_type=MESH
        )
    each(0, groups, lambda g: zcopy(g).start())
    pl.semaphore_wait(barrier, chips + nrow - 1)

    up = pltpu.make_async_remote_copy(
        basis.at[count - 1], halo.at[0], hsend.at[0], hrecv.at[0],
        device_id=(sub, (row + 1) % nrow), device_id_type=MESH,
    )
    down = pltpu.make_async_remote_copy(
        basis.at[0], halo.at[1], hsend.at[1], hrecv.at[1],
        device_id=(sub, (row + nrow - 1) % nrow), device_id_type=MESH,
    )

    @pl.when(row < nrow - 1)
    def _():
        up.start()

    @pl.when(row > 0)
    def _():
        down.start()

    each(0, groups, lambda g: zcopy(g).wait())
    def packet(turn, step):
        held = gath[turn]
        return pltpu.make_async_remote_copy(
            held.at[chip], held.at[chip], psend.at[turn, step], precv.at[turn, step],
            device_id=(((chip + step) % chips) * 2 + core, row), device_id_type=MESH,
        )

    def arrival(turn, step):
        held = gath[turn]
        source = (chip + chips - step) % chips
        return pltpu.make_async_remote_copy(
            held.at[source], held.at[source], psend.at[turn, step], precv.at[turn, step],
            device_id=(source * 2 + core, row), device_id_type=MESH,
        )

    def cross(turn):
        return pltpu.make_async_remote_copy(
            outbox[turn], inbox[turn], bsend.at[turn], brecv.at[turn],
            device_id=(mate, row), device_id_type=MESH,
        )

    for turn in range(rounds):
        for b in range(ovl):
            gath[turn][chip, b] = zpad[margins[b, turn] + 1]
        for step in range(1, chips):
            packet(turn, step).start()

    each(0, groups, lambda g: gcopy((g + 1) % groups).start())
    ccopy.start()

    acc[...] = jnp.zeros_like(acc)

    def work(g):
        first = g * GROUP
        parts = []
        for j in range(GROUP):
            near = zpad[pl.ds(first + j, 3)].reshape(3 * blk, width)
            image = jnp.dot(gbuf[first + j], near, preferred_element_type=jnp.float32)
            parts.append(split(image))
        own = zpad[pl.ds(first + 1, GROUP)].reshape(GROUP * blk, width)
        acc[...] += lax.dot_general(
            own, jnp.concatenate(parts, axis=0), TN, preferred_element_type=jnp.float32
        )

    def middle(g):
        gcopy(g).wait()
        work(g)

    def share_out(step, turn):
        there = (row + step) % nrow
        return pltpu.make_async_remote_copy(
            tsend.at[turn, there], trecv.at[turn, step - 1],
            tss.at[turn, step - 1], tsr.at[turn, step - 1],
            device_id=(sub, there), device_id_type=MESH,
        )

    def give(turn, both):
        tsend[turn] = (both[:, :width] + both[:, width:]).reshape(nrow, share, width)
        for step in range(1, nrow):
            share_out(step, turn).start()

    def collect(turn):
        total = tsend[turn, row]
        for step in range(1, nrow):
            share_out(step, turn).wait_recv()
            total += trecv[turn, step - 1]
        out[turn] = total

    def hand_over(turn):
        for step in range(1, chips):
            arrival(turn, step).wait_recv()
        wanted = partners[turn, mate] // 2
        for b in range(ovl):
            outbox[turn][b] = gath[turn][wanted, b]
        cross(turn).start()

    def couple(turn):
        wanted = partners[turn, sub]
        here = jnp.full((blk, width), wanted % 2, jnp.int32) == core
        parts = []
        cross(turn).wait_recv()
        for b in range(ovl):
            near = gath[turn][wanted // 2, b].astype(jnp.float32)
            far = inbox[turn][b].astype(jnp.float32)
            other = jnp.where(here, near, far).astype(jnp.bfloat16)
            parts.append(
                split(jnp.dot(cbuf[turn * ovl + b], other, preferred_element_type=jnp.float32))
            )
        own = gath[turn][chip].reshape(ovl * blk, width)
        give(turn + 1, lax.dot_general(
            own, jnp.concatenate(parts, axis=0), TN, preferred_element_type=jnp.float32
        ))

    def edges():
        @pl.when(row > 0)
        def _():
            up.wait_recv()
            zpad[0] = halo[0]

        @pl.when(row == 0)
        def _():
            zpad[0] = jnp.zeros((blk, width), jnp.bfloat16)

        @pl.when(row < nrow - 1)
        def _():
            down.wait_recv()
            zpad[count + 1] = halo[1]

        @pl.when(row == nrow - 1)
        def _():
            zpad[count + 1] = jnp.zeros((blk, width), jnp.bfloat16)

        each(0, 2, lambda i: middle(i * (groups - 1)))

    inner = groups - 2
    marks = [1 + inner * k // 10 for k in MARKS]
    each(1, marks[0], middle)
    ccopy.wait()
    for turn in range(rounds - 1):
        hand_over(turn)
        each(marks[2 * turn], marks[2 * turn + 1], middle)
        couple(turn)
        each(marks[2 * turn + 1], marks[2 * turn + 2], middle)
    each(marks[-1], groups - 1, middle)
    edges()
    give(0, acc[...])
    hand_over(rounds - 1)
    couple(rounds - 1)
    for turn in range(rounds):
        collect(turn)
    collect(rounds)

    @pl.when(row < nrow - 1)
    def _():
        up.wait_send()

    @pl.when(row > 0)
    def _():
        down.wait_send()

    for turn in range(rounds):
        for step in range(1, chips):
            packet(turn, step).wait_send()
        cross(turn).wait_send()
    for turn in range(rounds + 1):
        for step in range(1, nrow):
            share_out(step, turn).wait_send()


def local(nsub, nrow, basis, local_operator, coupling, partners, margin_blocks):
    rounds, _, _, ovl, blk, _ = coupling.shape
    rows, width = basis.shape[1:]
    count = rows // blk
    groups = count // GROUP
    share = width // nrow
    chips = nsub // 2
    bf16, f32 = jnp.bfloat16, jnp.float32
    dma = pltpu.SemaphoreType.DMA
    any_space = pl.BlockSpec(memory_space=pl.ANY)
    smem = pl.BlockSpec(memory_space=pltpu.SMEM)
    out = pl.pallas_call(
        functools.partial(kernel, nsub, nrow),
        out_shape=jax.ShapeDtypeStruct((1 + rounds, share, width), f32),
        in_specs=[smem, smem, any_space, any_space, any_space],
        out_specs=pl.BlockSpec(memory_space=pltpu.VMEM),
        scratch_shapes=[
            pltpu.VMEM((count + 2, blk, width), bf16),
            pltpu.VMEM((count, blk, 3 * blk), bf16),
            pltpu.VMEM((rounds * ovl, blk, blk), bf16),
            pltpu.VMEM((2, blk, width), bf16),
            [pltpu.VMEM((chips, ovl, blk, width), bf16) for _ in range(rounds)],
            [pltpu.VMEM((ovl, blk, width), bf16) for _ in range(rounds)],
            [pltpu.VMEM((ovl, blk, width), bf16) for _ in range(rounds)],
            pltpu.VMEM((width, 2 * width), f32),
            pltpu.VMEM((1 + rounds, nrow, share, width), f32),
            pltpu.VMEM((1 + rounds, nrow - 1, share, width), f32),
            dma((groups,)), dma((groups,)), dma(()), dma((2,)), dma((2,)),
            dma((rounds, chips)), dma((rounds, chips)), dma((rounds,)), dma((rounds,)),
            dma((1 + rounds, nrow - 1)), dma((1 + rounds, nrow - 1)),
        ],
        compiler_params=pltpu.CompilerParams(
            collective_id=0, has_side_effects=True, vmem_limit_bytes=56 << 20
        ),
        name="coarse",
    )(
        partners,
        margin_blocks[:, 0, 0].T,
        basis.reshape(count, blk, width),
        local_operator.reshape(count, blk, 3 * blk),
        coupling.reshape(rounds * ovl, blk, blk),
    )
    return out[None]


def solution(mesh):
    placed = (
        P("sub", "row", None),
        P("sub", "row", None),
        P(None, "sub", "row", None, None, None),
        P(),
        P(None, "sub", "row", None),
    )
    body = functools.partial(local, mesh.shape["sub"], mesh.shape["row"])
    return jax.shard_map(
        body, mesh=mesh, in_specs=placed, out_specs=P("sub", None, "row", None), check_vma=False
    )
```

```python
import functools

import jax
import jax.numpy as jnp
from jax import lax
from jax.experimental import pallas as pl
from jax.experimental.pallas import tpu as pltpu
from jax.sharding import PartitionSpec as P

MESH = pl.DeviceIdType.MESH
GROUP = 8
MARKS = (7, 8, 9, 10, 10)
TN = (((0,), (0,)), ((), ()))


def split(value):
    high = value.astype(jnp.bfloat16)
    low = (value - high.astype(jnp.float32)).astype(jnp.bfloat16)
    return jnp.concatenate([high, low], axis=1)


def kernel(
    nsub, nrow, partners, margins, basis, operator, coupling, out,
    zpad, gbuf, cbuf, halo, gath, outbox, inbox, acc,
    tsend, trecv,
    zsem, gsem, csem, hsend, hrecv, psend, precv, bsend, brecv,
    tss, tsr,
):
    sub = lax.axis_index("sub")
    row = lax.axis_index("row")
    chips = nsub // 2
    chip = sub // 2
    core = sub % 2
    mate = chip * 2 + (1 - core)
    count = basis.shape[0]
    groups = count // GROUP
    rounds = margins.shape[1]
    ovl = margins.shape[0]
    share = out.shape[1]
    blk = basis.shape[1]
    width = basis.shape[2]

    def zcopy(g):
        return pltpu.make_async_copy(
            basis.at[pl.ds(g * GROUP, GROUP)], zpad.at[pl.ds(g * GROUP + 1, GROUP)], zsem.at[g]
        )

    def gcopy(g):
        return pltpu.make_async_copy(
            operator.at[pl.ds(g * GROUP, GROUP)], gbuf.at[pl.ds(g * GROUP, GROUP)], gsem.at[g]
        )

    ccopy = pltpu.make_async_copy(coupling, cbuf, csem)

    def each(lower, upper, body):
        lax.fori_loop(lower, upper, lambda i, _: (body(i), 0)[1], 0)

    barrier = pltpu.get_barrier_semaphore()
    for step in range(1, chips):
        peer = ((chip + step) % chips) * 2 + core
        pl.semaphore_signal(barrier, inc=1, device_id=(peer, row), device_id_type=MESH)
    pl.semaphore_signal(barrier, inc=1, device_id=(mate, row), device_id_type=MESH)
    for step in range(1, nrow):
        pl.semaphore_signal(
            barrier, inc=1, device_id=(sub, (row + step) % nrow), device_id_type=MESH
        )
    each(0, groups, lambda g: zcopy(g).start())
    pl.semaphore_wait(barrier, chips + nrow - 1)

    up = pltpu.make_async_remote_copy(
        basis.at[count - 1], halo.at[0], hsend.at[0], hrecv.at[0],
        device_id=(sub, (row + 1) % nrow), device_id_type=MESH,
    )
    down = pltpu.make_async_remote_copy(
        basis.at[0], halo.at[1], hsend.at[1], hrecv.at[1],
        device_id=(sub, (row + nrow - 1) % nrow), device_id_type=MESH,
    )

    @pl.when(row < nrow - 1)
    def _():
        up.start()

    @pl.when(row > 0)
    def _():
        down.start()

    each(0, groups, lambda g: zcopy(g).wait())
    def packet(turn, step):
        held = gath[turn]
        return pltpu.make_async_remote_copy(
            held.at[chip], held.at[chip], psend.at[turn, step], precv.at[turn, step],
            device_id=(((chip + step) % chips) * 2 + core, row), device_id_type=MESH,
        )

    def arrival(turn, step):
        held = gath[turn]
        source = (chip + chips - step) % chips
        return pltpu.make_async_remote_copy(
            held.at[source], held.at[source], psend.at[turn, step], precv.at[turn, step],
            device_id=(source * 2 + core, row), device_id_type=MESH,
        )

    def cross(turn):
        return pltpu.make_async_remote_copy(
            outbox[turn], inbox[turn], bsend.at[turn], brecv.at[turn],
            device_id=(mate, row), device_id_type=MESH,
        )

    for turn in range(rounds):
        for b in range(ovl):
            gath[turn][chip, b] = zpad[margins[b, turn] + 1]
        for step in range(1, chips):
            packet(turn, step).start()

    each(0, groups, lambda g: gcopy((g + 1) % groups).start())
    ccopy.start()

    acc[...] = jnp.zeros_like(acc)

    def work(g):
        first = g * GROUP
        parts = []
        for j in range(GROUP):
            near = zpad[pl.ds(first + j, 3)].reshape(3 * blk, width)
            image = jnp.dot(gbuf[first + j], near, preferred_element_type=jnp.float32)
            parts.append(split(image))
        own = zpad[pl.ds(first + 1, GROUP)].reshape(GROUP * blk, width)
        acc[...] += lax.dot_general(
            own, jnp.concatenate(parts, axis=0), TN, preferred_element_type=jnp.float32
        )

    def middle(g):
        gcopy(g).wait()
        work(g)

    def share_out(step, turn):
        there = (row + step) % nrow
        return pltpu.make_async_remote_copy(
            tsend.at[turn, there], trecv.at[turn, step - 1],
            tss.at[turn, step - 1], tsr.at[turn, step - 1],
            device_id=(sub, there), device_id_type=MESH,
        )

    def give(turn, both):
        tsend[turn] = (both[:, :width] + both[:, width:]).reshape(nrow, share, width)
        for step in range(1, nrow):
            share_out(step, turn).start()

    def collect(turn):
        total = tsend[turn, row]
        for step in range(1, nrow):
            share_out(step, turn).wait_recv()
            total += trecv[turn, step - 1]
        out[turn] = total

    def hand_over(turn):
        for step in range(1, chips):
            arrival(turn, step).wait_recv()
        wanted = partners[turn, mate] // 2
        for b in range(ovl):
            outbox[turn][b] = gath[turn][wanted, b]
        cross(turn).start()

    def couple(turn):
        wanted = partners[turn, sub]
        here = jnp.full((blk, width), wanted % 2, jnp.int32) == core
        parts = []
        cross(turn).wait_recv()
        for b in range(ovl):
            near = gath[turn][wanted // 2, b].astype(jnp.float32)
            far = inbox[turn][b].astype(jnp.float32)
            other = jnp.where(here, near, far).astype(jnp.bfloat16)
            parts.append(
                split(jnp.dot(cbuf[turn * ovl + b], other, preferred_element_type=jnp.float32))
            )
        own = gath[turn][chip].reshape(ovl * blk, width)
        give(turn + 1, lax.dot_general(
            own, jnp.concatenate(parts, axis=0), TN, preferred_element_type=jnp.float32
        ))

    def edges():
        @pl.when(row > 0)
        def _():
            up.wait_recv()
            zpad[0] = halo[0]

        @pl.when(row == 0)
        def _():
            zpad[0] = jnp.zeros((blk, width), jnp.bfloat16)

        @pl.when(row < nrow - 1)
        def _():
            down.wait_recv()
            zpad[count + 1] = halo[1]

        @pl.when(row == nrow - 1)
        def _():
            zpad[count + 1] = jnp.zeros((blk, width), jnp.bfloat16)

        each(0, 2, lambda i: middle(i * (groups - 1)))

    inner = groups - 2
    marks = [1 + inner * k // 10 for k in MARKS]
    each(1, marks[0], middle)
    ccopy.wait()
    for turn in range(rounds - 1):
        hand_over(turn)
        each(marks[2 * turn], marks[2 * turn + 1], middle)
        couple(turn)
        each(marks[2 * turn + 1], marks[2 * turn + 2], middle)
    hand_over(rounds - 1)
    each(marks[-1], groups - 1, middle)
    edges()
    give(0, acc[...])
    couple(rounds - 1)
    for turn in range(rounds):
        collect(turn)
    collect(rounds)

    @pl.when(row < nrow - 1)
    def _():
        up.wait_send()

    @pl.when(row > 0)
    def _():
        down.wait_send()

    for turn in range(rounds):
        for step in range(1, chips):
            packet(turn, step).wait_send()
        cross(turn).wait_send()
    for turn in range(rounds + 1):
        for step in range(1, nrow):
            share_out(step, turn).wait_send()


def local(nsub, nrow, basis, local_operator, coupling, partners, margin_blocks):
    rounds, _, _, ovl, blk, _ = coupling.shape
    rows, width = basis.shape[1:]
    count = rows // blk
    groups = count // GROUP
    share = width // nrow
    chips = nsub // 2
    bf16, f32 = jnp.bfloat16, jnp.float32
    dma = pltpu.SemaphoreType.DMA
    any_space = pl.BlockSpec(memory_space=pl.ANY)
    smem = pl.BlockSpec(memory_space=pltpu.SMEM)
    out = pl.pallas_call(
        functools.partial(kernel, nsub, nrow),
        out_shape=jax.ShapeDtypeStruct((1 + rounds, share, width), f32),
        in_specs=[smem, smem, any_space, any_space, any_space],
        out_specs=pl.BlockSpec(memory_space=pltpu.VMEM),
        scratch_shapes=[
            pltpu.VMEM((count + 2, blk, width), bf16),
            pltpu.VMEM((count, blk, 3 * blk), bf16),
            pltpu.VMEM((rounds * ovl, blk, blk), bf16),
            pltpu.VMEM((2, blk, width), bf16),
            [pltpu.VMEM((chips, ovl, blk, width), bf16) for _ in range(rounds)],
            [pltpu.VMEM((ovl, blk, width), bf16) for _ in range(rounds)],
            [pltpu.VMEM((ovl, blk, width), bf16) for _ in range(rounds)],
            pltpu.VMEM((width, 2 * width), f32),
            pltpu.VMEM((1 + rounds, nrow, share, width), f32),
            pltpu.VMEM((1 + rounds, nrow - 1, share, width), f32),
            dma((groups,)), dma((groups,)), dma(()), dma((2,)), dma((2,)),
            dma((rounds, chips)), dma((rounds, chips)), dma((rounds,)), dma((rounds,)),
            dma((1 + rounds, nrow - 1)), dma((1 + rounds, nrow - 1)),
        ],
        compiler_params=pltpu.CompilerParams(
            collective_id=0, has_side_effects=True, vmem_limit_bytes=56 << 20
        ),
        name="coarse",
    )(
        partners,
        margin_blocks[:, 0, 0].T,
        basis.reshape(count, blk, width),
        local_operator.reshape(count, blk, 3 * blk),
        coupling.reshape(rounds * ovl, blk, blk),
    )
    return out[None]


def solution(mesh):
    placed = (
        P("sub", "row", None),
        P("sub", "row", None),
        P(None, "sub", "row", None, None, None),
        P(),
        P(None, "sub", "row", None),
    )
    body = functools.partial(local, mesh.shape["sub"], mesh.shape["row"])
    return jax.shard_map(
        body, mesh=mesh, in_specs=placed, out_specs=P("sub", None, "row", None), check_vma=False
    )
```
